256 devices in a mesh: gx: 16 (over z, x_hi), gy: 16 (over x_lo, y, core).
Axes of the slice: x: 4 (x_hi: 2, x_lo: 2; x = x_hi * 2 + x_lo), y: 4, z: 8, core: 2. Of those that a mesh axis runs over, the one named last changes fastest.
Arguments:
- tokens: bfloat16 [4096, 4096], P('gy', 'gx'), may hold values from -6 to 6
- attn_gain: bfloat16 [4096], replicated, may hold values from 0.099609375 to 1.8984375
- qkv_weight: bfloat16 [4096, 6144], P('gy', 'gx'), may hold values from -0.1875 to 0.1875
- out_weight: bfloat16 [4096, 4096], P('gx', 'gy'), may hold values from -0.09375 to 0.09375
- mlp_gain: bfloat16 [4096], replicated, may hold values from 0.099609375 to 1.8984375
- up_weight: bfloat16 [4096, 12288], P('gy', 'gx'), may hold values from -0.09375 to 0.09375
- down_weight: bfloat16 [12288, 4096], P('gx', 'gy'), may hold values from -0.0546875 to 0.0546875
- final_gain: bfloat16 [4096], replicated, may hold values from 0.099609375 to 1.8984375
- head_weight: bfloat16 [4096, 131072], P(None, ('gx', 'gy')), may hold values from -0.25 to 0.25
- kv_cache: bfloat16 [256, 4096, 256], P(('gy', 'gx')), may hold values from -40 to 40
- cache_lengths: int32 [32], replicated, may hold values from 1 to 3968, as said below
- slot_request: int32 [32], replicated, may hold values from 0 to 31, each once
Outputs:
- hidden_out: bfloat16 [4096, 4096], P('gy', 'gx')
- new_cache: bfloat16 [256, 4096, 256], P(('gy', 'gx'))
- last_norms: float32 [32], replicated
- max_logits: float32 [32], replicated
- head_input: bfloat16 [32, 4096], replicated
The draws below stay inside these ranges and needn't reach their ends.
Inputs may be any that keep to these rules, and one draw needn't show every extreme that they name: `cache_lengths`: the longest request has exactly 3968 cached positions.
All inputs are finite; a program needn't handle non-finite values.
Results may differ from the reference program's by a relative error of at most 0.02.
The reference program's roundings to bfloat16 on the way (of `normed`, `qkv_order`, `projected`, `attended`, `middle`, `mlp_input` and `activation`) count: a program that leaves them out, or rounds other values in their place, can miss the bound.
Values may be sent and summed in bfloat16 or wider, within the bound.
A program may use at most 128 MiB of HBM per device.

```python
import math
import jax
import jax.numpy as jnp
from jax import lax

D = 4096
HEADS = 32
KVH = 8
HD = 128
VOCAB = 131072
FF = 12288
CACHE = 4096
NEW = 128
COPIES = 2
SLOTS = 32
TOKENS = 4096
ATT = 4096
QKV = 6144


def draw_kv_cache(key, part):
    key_one = jax.random.fold_in(key, 0)
    values = 2.0 * jax.random.normal(key_one, (SLOTS * KVH, CACHE, 2 * HD), jnp.float32)
    return jnp.clip(values, -40.0, 40.0).astype(jnp.bfloat16)


def draw_cache_lengths(key, part):
    key_one, key_two, key_three = jax.random.split(key, 3)
    longest = CACHE - NEW
    first_draw = jax.random.randint(key_one, (SLOTS,), 1, longest + 1)
    second_draw = jax.random.randint(key_two, (SLOTS,), 1, longest + 1)
    skewed = jnp.maximum(first_draw * second_draw // longest, 1)
    chosen = jax.random.randint(key_three, (), 0, SLOTS)
    return jnp.where(jnp.arange(SLOTS) == chosen, longest, skewed).astype(jnp.int32)


def shard_levels(key, shape, cuts, least, largest):
    level, own = 1.0, jax.random.fold_in(key, 6)
    for axis_at, blocks in cuts:
        draws = jnp.exp(jax.random.uniform(jax.random.fold_in(own, axis_at), (blocks,), jnp.float32, least / len(cuts), largest / len(cuts)))
        level = level * jnp.repeat(draws, shape[axis_at] // blocks).reshape([-1 if axis == axis_at else 1 for axis in range(len(shape))])
    return level


def bell_draw(stream_key, shape, scale, limit, pieces=(), dtype=jnp.bfloat16):
    values = scale * jax.random.normal(stream_key, shape, jnp.float32)
    if pieces:
        values = values * shard_levels(stream_key, shape, pieces, -0.22, 0.18)
    return jnp.clip(values, -limit, limit).astype(dtype)


def setup_inputs(seed: int = 0) -> dict:
    key_list = jax.random.split(jax.random.key(seed), 13)
    return {
        "tokens": bell_draw(key_list[0], (TOKENS, D), 1.0, 6.0, ((0, 16), (1, 16))),
        "attn_gain": jnp.clip(1.0 + 0.18 * jax.random.normal(key_list[1], (D,), jnp.float32), 0.099609375, 1.8984375).astype(jnp.bfloat16),
        "qkv_weight": bell_draw(key_list[2], (D, QKV), (D // 4) ** -0.5, 0.1875, ((0, 16), (1, 16))),
        "out_weight": bell_draw(key_list[3], (ATT, D), ATT ** -0.5, 0.09375, ((0, 16), (1, 16))),
        "mlp_gain": jnp.clip(1.0 + 0.18 * jax.random.normal(key_list[4], (D,), jnp.float32), 0.099609375, 1.8984375).astype(jnp.bfloat16),
        "up_weight": bell_draw(key_list[5], (D, FF), D ** -0.5, 0.09375, ((0, 16), (1, 16))),
        "down_weight": bell_draw(key_list[6], (FF, D), FF ** -0.5, 0.0546875, ((0, 16), (1, 16))),
        "final_gain": jnp.clip(1.0 + 0.18 * jax.random.normal(key_list[7], (D,), jnp.float32), 0.099609375, 1.8984375).astype(jnp.bfloat16),
        "head_weight": bell_draw(key_list[8], (D, VOCAB), (D // 9) ** -0.5, 0.25, ((1, 256),)),
        "kv_cache": draw_kv_cache(jax.random.fold_in(key_list[12], 71), 0),
        "cache_lengths": draw_cache_lengths(jax.random.fold_in(key_list[12], 71), 0),
        "slot_request": jax.random.permutation(key_list[11], SLOTS).astype(jnp.int32),
    }


epsilon = 1e-05

def rms_factor(row_block):
    return lax.rsqrt(lax.optimization_barrier(jnp.mean(row_block * row_block, axis=-1, keepdims=True)) + epsilon)

def reference(tokens, attn_gain, qkv_weight, out_weight, mlp_gain, up_weight, down_weight, final_gain, head_weight, kv_cache, cache_lengths, slot_request):
    per_group = HEADS // KVH
    group_width = (per_group + 2) * HD
    qkv_piece = group_width // COPIES
    out_piece = per_group * HD // COPIES
    qkv_order = qkv_weight.reshape(D, COPIES, KVH, qkv_piece).transpose(0, 2, 1, 3).reshape(D, KVH * group_width)
    out_order = out_weight.reshape(COPIES, KVH, out_piece, D).transpose(1, 0, 2, 3).reshape(ATT, D)
    inputs_f32 = tokens.astype(jnp.float32)
    normed = (inputs_f32 * rms_factor(inputs_f32) * attn_gain.astype(jnp.float32)).astype(jnp.bfloat16)
    projected = jnp.dot(normed, qkv_order, preferred_element_type=jnp.float32).astype(jnp.bfloat16)
    per_slot = projected.reshape(SLOTS, NEW, KVH, group_width).transpose(0, 2, 1, 3).reshape(SLOTS * KVH, NEW, group_width)
    slot_lengths = jnp.repeat(cache_lengths[slot_request], KVH)
    scaling = 1.0 / math.sqrt(HD)
    query_token = jnp.arange(per_group * NEW) % NEW
    causal = jnp.arange(NEW)[None, :] <= query_token[:, None]
    cache_pos = jnp.arange(CACHE)

    def attend(item_parts):
        group_cols, cache_rows, length = item_parts
        queries = group_cols[:, :per_group * HD].reshape(NEW, per_group, HD).transpose(1, 0, 2).reshape(per_group * NEW, HD)
        key_new = group_cols[:, per_group * HD:(per_group + 1) * HD]
        value_new = group_cols[:, (per_group + 1) * HD:]
        cache_scores = jnp.dot(queries, cache_rows[:, :HD].T, preferred_element_type=jnp.float32) * scaling
        cache_scores = jnp.where(cache_pos[None, :] < length, cache_scores, -jnp.inf)
        new_scores = jnp.dot(queries, key_new.T, preferred_element_type=jnp.float32) * scaling
        new_scores = jnp.where(causal, new_scores, -jnp.inf)
        row_max = jnp.maximum(lax.optimization_barrier(jnp.max(cache_scores, axis=1, keepdims=True)), lax.optimization_barrier(jnp.max(new_scores, axis=1, keepdims=True)))
        cache_weights = jnp.exp(cache_scores - row_max)
        new_weights = jnp.exp(new_scores - row_max)
        denominator = lax.optimization_barrier(jnp.sum(cache_weights, axis=1, keepdims=True)) + lax.optimization_barrier(jnp.sum(new_weights, axis=1, keepdims=True))
        numerator = jnp.dot(cache_weights.astype(jnp.bfloat16), cache_rows[:, HD:], preferred_element_type=jnp.float32)
        numerator = numerator + jnp.dot(new_weights.astype(jnp.bfloat16), value_new, preferred_element_type=jnp.float32)
        attended = (numerator / denominator).astype(jnp.bfloat16)
        attended = attended.reshape(per_group, NEW, HD).transpose(1, 0, 2).reshape(NEW, per_group * HD)
        fresh = jnp.concatenate([key_new, value_new], axis=1)
        appended = lax.dynamic_update_slice(cache_rows, fresh, (length.astype(jnp.int32), jnp.zeros((), jnp.int32)))
        return (attended, appended)
    attended, new_cache = lax.map(attend, (per_slot, kv_cache, slot_lengths))
    attention = attended.reshape(SLOTS, KVH, NEW, per_group * HD).transpose(0, 2, 1, 3).reshape(TOKENS, ATT)
    middle_f32 = inputs_f32 + jnp.dot(attention, out_order, preferred_element_type=jnp.float32)
    middle = lax.optimization_barrier(middle_f32.astype(jnp.bfloat16))
    middle_in = middle.astype(jnp.float32)
    mlp_input = (middle_in * rms_factor(middle_in) * mlp_gain.astype(jnp.float32)).astype(jnp.bfloat16)
    up_values = jnp.dot(mlp_input, up_weight, preferred_element_type=jnp.float32)
    rectified = jnp.maximum(up_values, 0.0)
    activation = (rectified * rectified).astype(jnp.bfloat16)
    hidden_out = (middle_in + jnp.dot(activation, down_weight, preferred_element_type=jnp.float32)).astype(jnp.bfloat16)
    final_rows = hidden_out.reshape(SLOTS, NEW, D)[:, NEW - 1, :].astype(jnp.float32)
    mean_square = lax.optimization_barrier(jnp.mean(final_rows * final_rows, axis=1))
    last_norms = jnp.sqrt(mean_square)
    head_input = (final_rows * lax.rsqrt(mean_square + epsilon)[:, None] * final_gain.astype(jnp.float32)).astype(jnp.bfloat16)
    logits = jnp.dot(head_input, head_weight, preferred_element_type=jnp.float32)
    max_logits = lax.optimization_barrier(jnp.max(logits, axis=1))
    return (hidden_out, new_cache, last_norms, max_logits, head_input)
```

```python
import math

import jax
import jax.numpy as jnp
from jax import lax
from jax.experimental import pallas as pl
from jax.experimental.pallas import tpu as pltpu
from jax.sharding import PartitionSpec as P

HEADS = 32
KVH = 8
HD = 128
PER = HEADS // KVH
BF = jnp.bfloat16
F32 = jnp.float32

epsilon = 1e-05
negative = -1e30

GX = 16
GY = 16
NZ = 8
RIGHT_LIMIT = (4, 3)
LEFT_LIMIT = (3, 4)


class Copies:
    def __init__(self, send_sems, recv_sems):
        self.send_sems, self.recv_sems = send_sems, recv_sems
        self.names, self.sent = {}, []

    def index(self, name):
        return self.names.setdefault(name, len(self.names))

    def make(self, name, source, target, peer):
        at = self.index(name)
        return pltpu.make_async_remote_copy(
            src_ref=source,
            dst_ref=target,
            send_sem=self.send_sems.at[at],
            recv_sem=self.recv_sems.at[at],
            device_id=peer,
            device_id_type=pl.DeviceIdType.MESH,
        )

    def send(self, name, source, target, peer):
        copy = self.make(name, source, target, peer)
        copy.start()
        self.sent.append(copy)

    def arrive(self, name, target, peer):
        self.make(name, target, target, peer).wait_recv()

    def drain(self):
        for copy in self.sent:
            copy.wait_send()
        self.sent = []


def gx_at(dz, flip):
    place = lax.axis_index("gx")
    z, x = place // 2, place % 2
    return lax.rem(z + dz + NZ, NZ) * 2 + (1 - x if flip else x)


def gy_at(dx, dy, dc):
    place = lax.axis_index("gy")
    x, y, c = place // 8, (place // 2) % 4, place % 2
    return lax.rem(x + dx, 2) * 8 + lax.rem(y + dy + 4, 4) * 2 + lax.rem(c + dc, 2)


def gx_peer(dz, flip):
    return {"gx": gx_at(dz, flip)}


def gy_peer(dx, dy, dc):
    return {"gy": gy_at(dx, dy, dc)}


def greet(peers):
    barrier = pltpu.get_barrier_semaphore()
    for peer in peers:
        pl.semaphore_signal(barrier, inc=1, device_id=peer, device_id_type=pl.DeviceIdType.MESH)
    pl.semaphore_wait(barrier, len(peers))


GX_NEAR = ((1, 0), (-1, 0), (0, 1))
GY_NEAR = ((1, 0, 0), (0, 1, 0), (0, -1, 0), (0, 0, 1))


def gather_gx(copies, tag, own, slot, pieces, arrived):
    span = range(pieces)

    def push(way, flip, far, piece, source, origin):
        step = 1 if way == "R" else -1
        copies.send((tag, way, flip, far, piece), source, slot(origin, piece), gx_peer(step, 0))

    me = gx_at(0, 0)
    partner = gx_at(0, 1)
    for piece in span:
        push("R", 0, 1, piece, own(piece), me)
        push("L", 0, 1, piece, own(piece), me)
        copies.send((tag, "X", piece), own(piece), slot(me, piece), gx_peer(0, 1))
    yield

    def take(way, flip, far):
        limit = (RIGHT_LIMIT if way == "R" else LEFT_LIMIT)[flip]
        if far > limit:
            return
        origin = gx_at(-far if way == "R" else far, flip)
        for piece in span:
            here = slot(origin, piece)
            copies.arrive((tag, way, flip, far, piece), here, gx_peer(0, 1))
            if far < limit:
                push(way, flip, far + 1, piece, here, origin)
        for piece in span:
            arrived(origin, piece)

    for far in range(1, 6):
        take("R", 0, far)
        take("L", 0, far)
        yield
        if far == 1:
            for piece in span:
                here = slot(partner, piece)
                copies.arrive((tag, "X", piece), here, gx_peer(0, 1))
                push("R", 1, 1, piece, here, partner)
                push("L", 1, 1, piece, here, partner)
            for piece in span:
                arrived(partner, piece)
        else:
            take("R", 1, far - 1)
            take("L", 1, far - 1)
        yield


def gather_gy(copies, tag, own, slot):
    def push(name, source, origin, *step):
        copies.send((tag,) + name, source, slot(origin), gy_peer(*step))

    def share(dx, dy):
        origin = gy_at(dx, dy, 0)
        source = own if (dx, dy) == (0, 0) else slot(origin)
        push(("S", dx, dy % 4), source, origin, 0, 0, 1)

    def take(name, dx, dy):
        origin = gy_at(dx, dy, 0)
        here = slot(origin)
        copies.arrive((tag,) + name, here, gy_peer(0, 0, 1))
        return here, origin

    me = gy_at(0, 0, 0)
    push(("X",), own, me, 1, 0, 0)
    push(("U", 0, 1), own, me, 0, 1, 0)
    push(("D", 0, 1), own, me, 0, -1, 0)
    share(0, 0)
    yield
    here, origin = take(("X",), 1, 0)
    push(("U", 1, 1), here, origin, 0, 1, 0)
    push(("D", 1, 1), here, origin, 0, -1, 0)
    share(1, 0)
    yield
    here, origin = take(("U", 0, 1), 0, -1)
    push(("U", 0, 2), here, origin, 0, 1, 0)
    share(0, -1)
    take(("D", 0, 1), 0, 1)
    share(0, 1)
    yield
    here, origin = take(("D", 1, 1), 1, 1)
    push(("D", 1, 2), here, origin, 0, -1, 0)
    share(1, 1)
    take(("U", 1, 1), 1, -1)
    share(1, -1)
    yield
    take(("U", 0, 2), 0, -2)
    share(0, -2)
    take(("D", 1, 2), 1, 2)
    share(1, 2)
    yield
    for dx in (0, 1):
        for dy in range(4):
            copies.arrive((tag, "S", dx, dy), slot(gy_at(dx, dy, 1)), gy_peer(0, 0, 1))
    yield


def advance(*flows):
    for flow in flows:
        next(flow, None)


def finish(*flows):
    for flow in flows:
        for _ in flow:
            pass


def rows_at(index, count):
    return pl.ds(pl.multiple_of(index * count, count), count)


def square_sum(block):
    values = block.astype(F32)
    return jnp.sum(values * values, axis=1, keepdims=True)


def normalize(blocks, squares, gain, normed, width):
    factor = lax.rsqrt(squares[...] * (1.0 / (GX * width)) + epsilon)

    def one(at, _):
        columns = rows_at(at, width)
        values = blocks[at].astype(F32) * factor * gain[:, columns].astype(F32)
        normed[:, columns] = values.astype(BF)
        return _

    lax.fori_loop(0, GX, one, 0)


def project_kernel(
    tokens, gain, weight, out_shard, group, out_full,
    blocks, weights, out_mine, squares, normed, outgoing, incoming, send_sems, recv_sems, local_sem,
):
    rows, width = tokens.shape
    half = rows // 2
    depth = weight.shape[0]
    copies = Copies(send_sems, recv_sems)
    gx, gy = lax.axis_index("gx"), lax.axis_index("gy")
    turned = {"gx": gy, "gy": gx}
    diagonal = gx == gy
    greet(
        [gx_peer(*step) for step in GX_NEAR + ((4, 0),)]
        + [gy_peer(*step) for step in GY_NEAR]
        + [turned]
    )

    def slot(origin, piece):
        return blocks.at[origin]

    def arrived(origin, piece):
        squares[...] += square_sum(blocks[origin])

    feed = gather_gx(copies, "t", lambda piece: tokens, slot, 1, arrived)
    advance(feed)
    load = gather_gy(copies, "w", weight, lambda origin: weights.at[rows_at(origin, depth), :])
    advance(load)
    turn = copies.make(("turn",), out_shard, out_mine, turned)

    @pl.when(gx != gy)
    def _():
        turn.start()

    blocks[gx] = tokens[...]
    weights[rows_at(gy, depth), :] = weight[...]
    squares[...] = square_sum(tokens[...])

    @pl.when(diagonal)
    def _():
        out_mine[...] = out_shard[...]

    advance(feed)
    advance(feed)

    @pl.when(gx != gy)
    def _():
        turn.wait()

    def out_slot(origin):
        return out_full.at[rows_at(origin, depth), :]

    keep = pltpu.make_async_copy(out_mine, out_slot(gy), local_sem)
    keep.start()
    out_load = gather_gy(copies, "o", out_mine, out_slot)
    advance(load)
    advance(feed)
    advance(load)
    advance(feed)
    advance(load, out_load)
    for _ in feed:
        advance(load, out_load)
    finish(load)
    advance(out_load)

    normalize(blocks, squares, gain, normed, width)
    mine = gx // KVH
    outgoing[...] = jnp.dot(
        normed[rows_at(1 - mine, half), :], weights[...], preferred_element_type=F32
    ).astype(BF)
    copies.send(("swap",), outgoing, incoming, gx_peer(4, 0))
    group[mine] = jnp.dot(
        normed[rows_at(mine, half), :], weights[...], preferred_element_type=F32
    ).astype(BF)
    finish(out_load)
    copies.arrive(("swap",), incoming, gx_peer(4, 0))
    group[1 - mine] = incoming[...]
    keep.wait()
    copies.drain()


def attend_kernel(lengths, requests, group, cache, attended, new_cache, held, shifted, load_sem, store_sem, patch_sem):
    capacity = cache.shape[1]
    new = group.shape[1]
    queries = PER * new
    block = 512
    load = pltpu.make_async_copy(cache.at[0], held, load_sem)
    load.start()
    gx, gy = lax.axis_index("gx"), lax.axis_index("gy")
    slot = gy * 2 + gx // KVH
    length = lengths[requests[slot]]
    scaling = 1.0 / math.sqrt(HD)
    query = jnp.concatenate(
        [group[0, :, 0:HD], group[0, :, HD : 2 * HD], group[0, :, 2 * HD :], group[1, :, 0:HD]], axis=0
    )
    fresh = group[1, :, HD:]
    window = shifted.shape[0]
    base = pl.multiple_of(jnp.minimum(length // 16 * 16, capacity - window), 16)
    offset = length - base
    at = lax.broadcasted_iota(jnp.int32, (window, new), 0)
    token = lax.broadcasted_iota(jnp.int32, (window, new), 1)
    pick = jnp.where(at == token + offset, 1.0, 0.0).astype(BF)
    moved = jnp.dot(pick, fresh, preferred_element_type=F32)
    row = lax.broadcasted_iota(jnp.int32, (window, 2 * HD), 0)
    inside = jnp.logical_and(row >= offset, row < offset + new)
    load.wait()
    shifted[...] = jnp.where(inside, moved, held[pl.ds(base, window), :].astype(F32)).astype(BF)
    held[pl.ds(base, window), :] = shifted[...]
    store = pltpu.make_async_copy(held, new_cache.at[0], store_sem)
    store.start()

    key_at = lax.broadcasted_iota(jnp.int32, (block, queries), 0)
    ahead = key_at - lax.rem(lax.broadcasted_iota(jnp.int32, (block, queries), 1), new)

    def visit(step, carried):
        top, total, numerator = carried
        keys = rows_at(step, block)
        scores = lax.dot_general(
            held[keys, 0:HD], query, (((1,), (1,)), ((), ())), preferred_element_type=F32
        ) * scaling
        scores = jnp.where(ahead + step * block <= length, scores, negative)
        new_top = jnp.maximum(top, jnp.max(scores, axis=0, keepdims=True))
        factor = jnp.exp(top - new_top)
        weights = jnp.exp(scores - new_top)
        total = total * factor + jnp.sum(weights, axis=0, keepdims=True)
        numerator = numerator * factor + lax.dot_general(
            held[keys, HD:], weights.astype(BF), (((0,), (0,)), ((), ())), preferred_element_type=F32
        )
        return new_top, total, numerator

    initial = (
        jnp.full((1, queries), negative, F32),
        jnp.zeros((1, queries), F32),
        jnp.zeros((HD, queries), F32),
    )
    steps = (length + new + block - 1) // block
    top, total, numerator = lax.fori_loop(0, steps, visit, initial)
    result = numerator / total
    for head in range(PER):
        columns = slice(head % 2 * HD, head % 2 * HD + HD)
        attended[head // 2, :, columns] = result[:, head * new : (head + 1) * new].T.astype(BF)
    store.wait()


def feed_kernel(
    tokens, attended, out_full, gain, up_shard, down_shard, hidden, last,
    gathered, out_w, up_w, down_w, middle, blocks, squares, normed, active, stage, landing, crossing,
    partial, total, own_last, lasts, send_sems, recv_sems, local_sems,
):
    rows, width = tokens.shape
    half = rows // 2
    copies = Copies(send_sems, recv_sems)
    gx, gy = lax.axis_index("gx"), lax.axis_index("gy")
    greet([gx_peer(*step) for step in GX_NEAR] + [gy_peer(*step) for step in GY_NEAR])

    def att_slot(origin, piece):
        return gathered.at[piece * KVH + lax.rem(origin, KVH), rows_at(origin // KVH, half), :]

    flow = gather_gx(copies, "a", lambda piece: attended.at[piece], att_slot, 2, lambda origin, piece: None)
    advance(flow)
    depth = up_shard.shape[0]
    up_load = gather_gy(copies, "u", up_shard, lambda origin: up_w.at[rows_at(origin, depth), :])
    down_load = gather_gy(copies, "d", down_shard, lambda origin: down_w.at[origin])
    advance(up_load)
    fetch = pltpu.make_async_copy(out_full, out_w, local_sems.at[0])
    fetch.start()
    keep_up = pltpu.make_async_copy(up_shard, up_w.at[rows_at(gy, depth), :], local_sems.at[1])
    keep_up.start()
    keep_down = pltpu.make_async_copy(down_shard, down_w.at[gy], local_sems.at[2])
    keep_down.start()
    for piece in range(2):
        gathered[piece * KVH + lax.rem(gx, KVH), rows_at(gx // KVH, half), :] = attended[piece]
    for count, _ in enumerate(flow):
        if count == 4:
            advance(up_load, down_load)
        if count == 6:
            advance(up_load)
        if count == 8:
            advance(up_load, down_load)
    fetch.wait()
    sums = tokens[...].astype(F32)
    acc = jnp.zeros((rows, width), F32)
    for at in range(GX):
        acc = acc + jnp.dot(
            gathered[at], out_w[at * width : (at + 1) * width, :], preferred_element_type=F32
        )
    middle[...] = (sums + acc).astype(BF)

    def mid_slot(origin, piece):
        return blocks.at[origin, piece * half : (piece + 1) * half, :]

    def arrived(origin, piece):
        part = slice(piece * half, (piece + 1) * half)
        squares[part, :] += square_sum(blocks[origin, part, :])

    flow = gather_gx(copies, "m", lambda piece: middle.at[piece * half : (piece + 1) * half, :], mid_slot, 2, arrived)
    advance(flow)
    blocks[gx] = middle[...]
    squares[...] = square_sum(middle[...])
    for count, _ in enumerate(flow):
        if count == 1:
            advance(up_load, down_load)
        if count == 4:
            advance(up_load, down_load)
        if count == 6:
            advance(down_load)
    finish(up_load)
    normalize(blocks, squares, gain, normed, width)
    keep_up.wait()

    def unit(at, _):
        columns = rows_at(at, width)
        values = jnp.dot(normed[...], up_w[:, columns], preferred_element_type=F32)
        values = jnp.maximum(values, 0.0)
        active[:, columns] = (values * values).astype(BF)
        return _

    lax.fori_loop(0, active.shape[1] // width, unit, 0)
    keep_down.wait()
    finish(down_load)

    def share(origin):
        return jnp.dot(active[...], down_w[origin], preferred_element_type=F32)

    chains = (("L", 1, 4), ("R", 1, 3), ("R", 0, 4), ("L", 0, 3))
    spots = {}
    for way, flip, limit in chains:
        for left in range(limit):
            spots[way, flip, left] = len(spots)

    def toward(way, flip, left):
        return gx_at(left if way == "R" else -left, flip)

    def pass_on(way, flip, left, source):
        copies.send(
            ("r", way, flip, left),
            source,
            landing.at[spots[way, flip, left - 1]],
            gx_peer(1 if way == "R" else -1, 0),
        )

    for at, (way, flip, limit) in enumerate(chains):
        stage[at] = share(toward(way, flip, limit)).astype(BF)
        pass_on(way, flip, limit, stage.at[at])
    total[1] = share(gx_at(0, 1))
    total[0] = share(gx) + middle[...].astype(F32)
    for turn in range(1, 5):
        for way, flip, limit in chains:
            left = limit - turn
            if left < 0:
                continue
            spot = spots[way, flip, left]
            if left > 0:
                partial[...] = share(toward(way, flip, left))
            copies.arrive(("r", way, flip, left + 1), landing.at[spot], gx_peer(0, 1))
            if left > 0:
                landing[spot] = (landing[spot].astype(F32) + partial[...]).astype(BF)
                pass_on(way, flip, left, landing.at[spot])
            else:
                total[flip] += landing[spot].astype(F32)
                if (way, flip) == ("L", 1):
                    crossing[0] = total[1].astype(BF)
                    copies.send(("r", "X"), crossing.at[0], crossing.at[1], gx_peer(0, 1))
    copies.arrive(("r", "X"), crossing.at[1], gx_peer(0, 1))
    result = (total[0] + crossing[1].astype(F32)).astype(BF)
    hidden[...] = result
    total[0] = result.astype(F32)
    lane = width // 2
    for slot in range(2):
        for side in range(2):
            last[2 * slot + side : 2 * slot + side + 1, :] = total[
                0, slot * half + half - 1 : slot * half + half, side * lane : (side + 1) * lane
            ]
    copies.drain()


def spread_kernel(own, result, row, send_sems, recv_sems):
    copies = Copies(send_sems, recv_sems)
    gx, gy = lax.axis_index("gx"), lax.axis_index("gy")
    xs = [lax.rem(gx + step, GX) for step in range(1, GX)]
    ys = [lax.rem(gy + step, GY) for step in range(1, GY)]
    greet([{"gx": at} for at in xs] + [{"gy": at} for at in ys])
    for step, at in enumerate(xs):
        copies.send(("x", step), own, row.at[gx], {"gx": at})
    row[gx] = own[...]
    for step in range(GX - 1):
        copies.arrive(("x", step), row.at[lax.rem(gx + GX - 1 - step, GX)], {"gx": xs[0]})
    for step, at in enumerate(ys):
        copies.send(("y", step), row, result.at[gy], {"gy": at})
    result[gy] = row[...]
    for step in range(GY - 1):
        copies.arrive(("y", step), result.at[lax.rem(gy + GY - 1 - step, GY)], {"gy": ys[0]})
    copies.drain()


def largest_kernel(own, result, row, column, best, send_sems, recv_sems):
    copies = Copies(send_sems, recv_sems)
    gx, gy = lax.axis_index("gx"), lax.axis_index("gy")
    xs = [lax.rem(gx + step, GX) for step in range(1, GX)]
    ys = [lax.rem(gy + step, GY) for step in range(1, GY)]
    greet([{"gx": at} for at in xs] + [{"gy": at} for at in ys])
    for step, at in enumerate(ys):
        copies.send(("y", step), own, column.at[gy], {"gy": at})
    column[gy] = own[...]
    for step in range(GY - 1):
        copies.arrive(("y", step), column.at[lax.rem(gy + GY - 1 - step, GY)], {"gy": ys[0]})
    best[...] = jnp.max(column[...], axis=0)
    for step, at in enumerate(xs):
        copies.send(("x", step), best, row.at[gx], {"gx": at})
    row[gx] = best[...]
    for step in range(GX - 1):
        copies.arrive(("x", step), row.at[lax.rem(gx + GX - 1 - step, GX)], {"gx": xs[0]})
    result[...] = jnp.max(row[...], axis=0)
    copies.drain()


VM = pl.BlockSpec(memory_space=pltpu.VMEM)
SM = pl.BlockSpec(memory_space=pltpu.SMEM)
ANY = pl.BlockSpec(memory_space=pl.ANY)


def sems(count):
    return [pltpu.SemaphoreType.DMA((count,)), pltpu.SemaphoreType.DMA((count,))]


def params(collective):
    return pltpu.CompilerParams(collective_id=collective, has_side_effects=True)


def local(
    tokens,
    attn_gain,
    qkv_weight,
    out_weight,
    mlp_gain,
    up_weight,
    down_weight,
    final_gain,
    head_weight,
    kv_cache,
    cache_lengths,
    slot_request,
):
    rows, width = tokens.shape
    half = rows // 2
    model = GX * width
    columns = qkv_weight.shape[1]
    units = up_weight.shape[1]
    shape = jax.ShapeDtypeStruct
    group, out_full = pl.pallas_call(
        project_kernel,
        name="project",
        out_shape=[shape((2, half, columns), BF), shape((model, width), BF)],
        in_specs=[VM] * 4,
        out_specs=[VM, ANY],
        scratch_shapes=[
            pltpu.VMEM((GX, rows, width), BF),
            pltpu.VMEM((model, columns), BF),
            pltpu.VMEM((width, width), BF),
            pltpu.VMEM((rows, 1), F32),
            pltpu.VMEM((rows, model), BF),
            pltpu.VMEM((half, columns), BF),
            pltpu.VMEM((half, columns), BF),
        ]
        + sems(50)
        + [pltpu.SemaphoreType.DMA(())],
        compiler_params=params(0),
    )(tokens, attn_gain[None], qkv_weight, out_weight)
    window = half + 16
    attended, new_cache = pl.pallas_call(
        attend_kernel,
        name="attend",
        out_shape=[shape((2, half, 2 * HD), BF), shape(kv_cache.shape, BF)],
        in_specs=[SM, SM, VM, ANY],
        out_specs=[VM, ANY],
        scratch_shapes=[
            pltpu.VMEM(kv_cache.shape[1:], BF),
            pltpu.VMEM((window, 2 * HD), BF),
            pltpu.SemaphoreType.DMA(()),
            pltpu.SemaphoreType.DMA(()),
            pltpu.SemaphoreType.DMA(()),
        ],
    )(cache_lengths, slot_request, group, kv_cache)
    hidden_out, last = pl.pallas_call(
        feed_kernel,
        name="feed",
        out_shape=[shape((rows, width), BF), shape((4, width // 2), F32)],
        in_specs=[VM, VM, ANY, VM, VM, VM],
        out_specs=[VM, VM],
        scratch_shapes=[
            pltpu.VMEM((GX, rows, width), BF),
            pltpu.VMEM((model, width), BF),
            pltpu.VMEM((model, units), BF),
            pltpu.VMEM((GX, units, width), BF),
            pltpu.VMEM((rows, width), BF),
            pltpu.VMEM((GX, rows, width), BF),
            pltpu.VMEM((rows, 1), F32),
            pltpu.VMEM((rows, model), BF),
            pltpu.VMEM((rows, units), BF),
            pltpu.VMEM((4, rows, width), BF),
            pltpu.VMEM((14, rows, width), BF),
            pltpu.VMEM((2, rows, width), BF),
            pltpu.VMEM((rows, width), F32),
            pltpu.VMEM((2, rows, width), F32),
            pltpu.VMEM((4, width // 2), F32),
            pltpu.VMEM((8, width // 2), F32),
        ]
        + sems(110)
        + [pltpu.SemaphoreType.DMA((3,))],
        compiler_params=params(1),
    )(tokens, attended, out_full, mlp_gain[None], up_weight, down_weight)
    every_last = pl.pallas_call(
        spread_kernel,
        name="spread",
        out_shape=shape((GY, GX, 4, width // 2), F32),
        in_specs=[VM],
        out_specs=VM,
        scratch_shapes=[pltpu.VMEM((GX, 4, width // 2), F32)] + sems(30),
        compiler_params=params(2),
    )(last)
    slot_rows = every_last.reshape(GY, GX, 2, width).transpose(0, 2, 1, 3).reshape(2 * GY, model)
    mean_square = jnp.mean(slot_rows * slot_rows, axis=1)
    last_norms = jnp.sqrt(mean_square)
    head_input = (
        slot_rows * lax.rsqrt(mean_square + epsilon)[:, None] * final_gain.astype(F32)
    ).astype(BF)
    logits = jnp.dot(head_input, head_weight, preferred_element_type=F32)
    own_best = jnp.pad(jnp.max(logits, axis=1), (0, 128 - 2 * GY))[None]
    best = pl.pallas_call(
        largest_kernel,
        name="largest",
        out_shape=shape((1, 128), F32),
        in_specs=[VM],
        out_specs=VM,
        scratch_shapes=[
            pltpu.VMEM((GX, 1, 128), F32),
            pltpu.VMEM((GY, 1, 128), F32),
            pltpu.VMEM((1, 128), F32),
        ]
        + sems(30),
        compiler_params=params(3),
    )(own_best)
    max_logits = best[0, : 2 * GY]
    return (hidden_out, new_cache, last_norms, max_logits, head_input)


def solution(mesh):
    in_specs = (
        P("gy", "gx"),
        P(),
        P("gy", "gx"),
        P("gx", "gy"),
        P(),
        P("gy", "gx"),
        P("gx", "gy"),
        P(),
        P(None, ("gx", "gy")),
        P(("gy", "gx"), None, None),
        P(),
        P(),
    )
    out_specs = (P("gy", "gx"), P(("gy", "gx"), None, None), P(), P(), P())
    return jax.shard_map(local, mesh=mesh, in_specs=in_specs, out_specs=out_specs, check_vma=False)
```
